128 devices in a mesh: grp: 8 (over z, x_hi), dev: 16 (over y, x_lo, core).
Axes of the slice: x: 4 (x_hi: 2, x_lo: 2; x = x_hi * 2 + x_lo), y: 4, z: 4, core: 2. Of those that a mesh axis runs over, the one named last changes fastest.
Arguments:
- output_gradient: bfloat16 [16384, 2048], P(('grp', 'dev')), may hold values from -6 to 6
- expert_choice_index: int32 [16384, 8], P(('grp', 'dev')), may hold values from 0 to 127, all different within a row; in each aligned block of 128 rows (0 to 127, 128 to 255, ...) at most 10 rows name the same one
- routing_weight: float32 [16384, 8], P(('grp', 'dev')), may hold values from 0.05 to 0.3
- stored_gate_preact: bfloat16 [128, 1280, 1536], P(('grp', 'dev')), may hold values from -6 to 6
- gate_up_weight: bfloat16 [128, 2048, 1536], P(('grp', 'dev')), may hold values from -0.125 to 0.125
- down_weight: bfloat16 [128, 768, 2048], P(('grp', 'dev')), may hold values from -0.21875 to 0.21875
- down_first_factor: bfloat16 [128, 64, 768], P(('grp', 'dev')), may hold values from -0.21875 to 0.21875
- down_second_factor: bfloat16 [128, 64, 2048], P(('grp', 'dev')), may hold values from -0.75 to 0.75
- rotated_queries: bfloat16 [16384, 4096], P('grp', 'dev'), may hold values from -800 to 800
- rotated_keys: bfloat16 [16384, 512], P('grp'), may hold values from -4 to 4
- stored_values: bfloat16 [16384, 512], P('grp'), may hold values from -6 to 6
- output_weight: bfloat16 [4096, 2048], P('dev'), may hold values from -0.09375 to 0.09375
- output_first_factor: bfloat16 [64, 4096], P(None, 'dev'), may hold values from -0.09375 to 0.09375
- output_second_factor: bfloat16 [64, 2048], replicated, may hold values from -0.75 to 0.75
Outputs:
- first_factor_gradient: float32 [128, 64, 768], P(('grp', 'dev'))
- second_factor_gradient: float32 [128, 64, 2048], P(('grp', 'dev'))
- residual_gradient: bfloat16 [16384, 2048], P(('grp', 'dev'))
- output_first_gradient: float32 [64, 4096], P(None, 'dev')
- output_second_gradient: float32 [64, 2048], replicated
- query_gradient: float32 [16384, 4096], P('grp', 'dev')
- key_gradient: float32 [16384, 512], P(('grp', 'dev'))
- value_gradient: float32 [16384, 512], P(('grp', 'dev'))
The draws below stay inside these ranges and needn't reach their ends.
Inputs may be any that keep to these rules, and one draw needn't show every extreme that they name: `expert_choice_index`: each row names 8 different experts; within the rows of one device no expert is named more than 10 times, a bound that some block reaches.
All inputs are finite; a program needn't handle non-finite values.
Results may differ from the reference program's by a relative error of at most 0.024.
Values may be sent and summed in bfloat16 or wider, within the bound.
A program may use at most 192 MiB of HBM per device.

```python
import math
import jax
import jax.numpy as jnp
import numpy as np
from jax import lax

MODEL_DIM = 2048
FFN_HIDDEN = 768
QUERY_HEADS = 32
KVH = 4
HEAD_SIZE = 128
TOP = 8
ADAPTER_RANK = 64
TOK_DEV = 128
PIECE = 2048
TOKEN_TOTAL = 16384
EXPERT_COUNT = 128
CAP = 10
SLOTS = 1280
N_GRP = 8


def paired_states(key):
    shape_k = (TOKEN_TOTAL, KVH, HEAD_SIZE)
    shape_q = (TOKEN_TOTAL, QUERY_HEADS, HEAD_SIZE)
    base_k = jax.random.normal(jax.random.fold_in(key, 11), shape_k, jnp.float32)
    base_q = jax.random.normal(jax.random.fold_in(key, 12), shape_q, jnp.float32)
    base_k = jnp.clip(base_k, -4.0, 4.0)
    base_q = jnp.clip(base_q, -4.0, 4.0)
    return (base_q, base_k)


def draw_rotated_queries(key, part):
    base_q, base_k = paired_states(key)
    return base_q.reshape(TOKEN_TOTAL, QUERY_HEADS * HEAD_SIZE).astype(jnp.bfloat16)


def draw_rotated_keys(key, part):
    base_q, base_k = paired_states(key)
    return base_k.reshape(TOKEN_TOTAL, KVH * HEAD_SIZE).astype(jnp.bfloat16)


def steps_of(rng, shape, split, low, largest):
    def one(dim, shards_of):
        heights = jax.random.uniform(jax.random.fold_in(jax.random.fold_in(rng, 6), dim), (shards_of,), jnp.float32, low / len(split), largest / len(split))
        return jnp.repeat(jnp.exp(heights), shape[dim] // shards_of).reshape((-1,) + (1,) * (len(shape) - dim - 1))

    factor_of = one(*split[0])
    for cut in split[1:]:
        factor_of = factor_of * one(*cut)
    return factor_of


def shared_out(stream_key, own, number, rows, amount, top, bound, lean):
    ranking = jax.random.permutation(stream_key, amount)
    crowded, common = portions_of(amount, rows * top, bound, lean, True), portions_of(amount, rows * top, bound, lean, False)
    places = jnp.arange(amount)

    def named(tallies, rotation):
        used = int((tallies > 0).sum())
        fixed = max(1, used // 4)
        moved = fixed + (places - fixed + rotation * (used - fixed)) % max(1, amount - fixed)
        return jnp.zeros((amount,), jnp.int32).at[ranking[jnp.where(places < fixed, places, moved)]].set(jnp.asarray(tallies, jnp.int32))

    tallies = jnp.where(number % 4 == 0, named(crowded, number // 4), named(common, number - number // 4 - 1))
    mixed = jax.random.permutation(jax.random.fold_in(own, 3), amount)
    source_of, receiver = mixed[0:amount // 2 * 2:2], mixed[1:amount // 2 * 2:2]
    room = jnp.minimum(tallies[source_of] - 1, bound - tallies[receiver]) // 2
    room = jnp.where((source_of == ranking[0]) | (receiver == ranking[0]) | (tallies[receiver] == 0), 0, jnp.maximum(room, 0))
    moved = jax.random.randint(jax.random.fold_in(own, 4), (amount // 2,), 0, 1 << 20) % (room + 1)
    tallies = tallies.at[source_of].add(-moved).at[receiver].add(moved)
    members = jnp.searchsorted(jnp.cumsum(tallies), jnp.arange(rows * top), side="right").astype(jnp.int32)
    grid = members.reshape(top, rows).T
    grid = grid[jax.random.permutation(jax.random.fold_in(own, 1), rows)]
    rotation = jax.random.randint(jax.random.fold_in(own, 2), (rows, 1), 0, top)
    return jnp.take_along_axis(grid, (jnp.arange(top)[None, :] + rotation) % top, axis=1)


def portions_of(amount, total, reach, skew, full):
    weights = [(1 << 20) // math.isqrt(standing ** skew) + 1 for standing in range(1, amount + 1)]
    largest = reach if full else min(reach, max(-(-total // amount), total * weights[0] // sum(weights)))
    least = 1 if total - largest >= amount - 1 else 0
    holding, rest = [largest] + [least] * (amount - 1), total - largest - least * (amount - 1)
    while rest > 0:
        candidates = [i for i in range(1, amount) if holding[i] < largest] or [i for i in range(1, amount) if holding[i] < reach]
        pool, remaining = sum([weights[i] for i in candidates]), rest
        for i in candidates:
            more = min(reach - holding[i], max(1, remaining * weights[i] // pool), rest)
            holding[i] = holding[i] + more
            rest = rest - more
    return np.array(holding)


def normal_values(own_key, extent, spread, reach, shards=(), kind=jnp.bfloat16):
    level = steps_of(own_key, extent, shards, -0.22, 0.18) if shards else 1.0
    entries = jax.random.normal(own_key, extent, jnp.float32) * spread * level
    return jnp.minimum(jnp.maximum(entries, -reach), reach).astype(kind)


def setup_inputs(seed: int = 0) -> dict:
    streams_of = jax.random.split(jax.random.key(seed), 15)
    output_gradient = normal_values(streams_of[0], (TOKEN_TOTAL, MODEL_DIM), 1.0, 6.0, ((0, 128),))
    expert_choice_index_keys = jax.random.split(jax.random.fold_in(streams_of[1], 1), TOKEN_TOTAL // TOK_DEV)
    expert_choice_index_turns = jax.random.permutation(jax.random.fold_in(streams_of[1], 3), TOKEN_TOTAL // TOK_DEV)
    expert_choice_index = jax.vmap(lambda own, number: shared_out(jax.random.fold_in(streams_of[1], 2), own, number, TOK_DEV, EXPERT_COUNT, TOP, CAP, 2))(expert_choice_index_keys, expert_choice_index_turns).reshape((TOKEN_TOTAL, TOP))
    routing_weight = jnp.clip(0.05 + 0.25 * jax.random.uniform(streams_of[2], (TOKEN_TOTAL, TOP), jnp.float32) ** steps_of(streams_of[2], (TOKEN_TOTAL, TOP), ((0, 128),), -0.2, 0.2), 0.05, 0.3)
    stored_gate_preact = normal_values(streams_of[3], (EXPERT_COUNT, SLOTS, 2 * FFN_HIDDEN), 1.0, 6.0, ((0, 128),))
    gate_up_weight = normal_values(streams_of[4], (EXPERT_COUNT, MODEL_DIM, 2 * FFN_HIDDEN), MODEL_DIM ** -0.5, 0.125, ((0, 128),))
    down_weight = normal_values(streams_of[5], (EXPERT_COUNT, FFN_HIDDEN, MODEL_DIM), FFN_HIDDEN ** -0.5, 0.21875, ((0, 128),))
    down_first_factor = normal_values(streams_of[6], (EXPERT_COUNT, ADAPTER_RANK, FFN_HIDDEN), FFN_HIDDEN ** -0.5, 0.21875, ((0, 128),))
    down_second_factor = normal_values(streams_of[7], (EXPERT_COUNT, ADAPTER_RANK, MODEL_DIM), ADAPTER_RANK ** -0.5, 0.75, ((0, 128),))
    rotated_queries = draw_rotated_queries(jax.random.fold_in(streams_of[14], 71), 0)
    rotated_keys = draw_rotated_keys(jax.random.fold_in(streams_of[14], 71), 0)
    stored_values = normal_values(streams_of[10], (TOKEN_TOTAL, KVH * HEAD_SIZE), 1.0, 6.0, ((0, 8),))
    output_weight = normal_values(streams_of[11], (QUERY_HEADS * HEAD_SIZE, MODEL_DIM), (QUERY_HEADS * HEAD_SIZE) ** -0.5, 0.09375, ((0, 16),))
    output_first_factor = normal_values(streams_of[12], (ADAPTER_RANK, QUERY_HEADS * HEAD_SIZE), (QUERY_HEADS * HEAD_SIZE) ** -0.5, 0.09375, ((1, 16),))
    output_second_factor = normal_values(streams_of[13], (ADAPTER_RANK, MODEL_DIM), ADAPTER_RANK ** -0.5, 0.75)
    return dict(output_gradient=output_gradient, expert_choice_index=expert_choice_index, routing_weight=routing_weight, stored_gate_preact=stored_gate_preact, gate_up_weight=gate_up_weight, down_weight=down_weight, down_first_factor=down_first_factor, down_second_factor=down_second_factor, rotated_queries=rotated_queries, rotated_keys=rotated_keys, stored_values=stored_values, output_weight=output_weight, output_first_factor=output_first_factor, output_second_factor=output_second_factor)


adapter_scale = 2.0
neg_big = -1e30


def expert_backward(routed_rows, saved_rows, gate_up, down_output, lowrank_first, low_b):
    pre_gate = saved_rows[:, :FFN_HIDDEN].astype(jnp.float32)
    pre_up = saved_rows[:, FFN_HIDDEN:].astype(jnp.float32)
    sigmoid = jax.nn.sigmoid(pre_gate)
    activated = pre_gate * sigmoid
    slope = sigmoid * (1.0 + pre_gate * (1.0 - sigmoid))
    hidden_activity = (activated * pre_up).astype(jnp.bfloat16)
    lowrank_input = jnp.dot(hidden_activity, lowrank_first.T, preferred_element_type=jnp.float32).astype(jnp.bfloat16)
    lowrank_gradient = jnp.dot(routed_rows, low_b.T, preferred_element_type=jnp.float32).astype(jnp.bfloat16)
    gradient_second = adapter_scale * jnp.dot(lowrank_input.T, routed_rows, preferred_element_type=jnp.float32)
    gradient_first = adapter_scale * jnp.dot(lowrank_gradient.T, hidden_activity, preferred_element_type=jnp.float32)
    hidden_gradient = jnp.dot(routed_rows, down_output.T, preferred_element_type=jnp.float32) + adapter_scale * jnp.dot(lowrank_gradient, lowrank_first, preferred_element_type=jnp.float32)
    grad_pre = jnp.concatenate([hidden_gradient * pre_up * slope, hidden_gradient * activated], axis=1).astype(jnp.bfloat16)
    grad_rows = jnp.dot(grad_pre, gate_up.T, preferred_element_type=jnp.float32).astype(jnp.bfloat16)
    return grad_rows, gradient_first, gradient_second


def head_backward(query_rows, key_rows, value_rows, grad_rows):
    att_scale = HEAD_SIZE ** -0.5
    scores = jnp.dot(query_rows, key_rows.T, preferred_element_type=jnp.float32) * att_scale
    positions = jnp.arange(PIECE, dtype=jnp.int32)
    scores = jnp.where(positions[:, None] >= positions[None, :], scores, neg_big)
    probs_full = jnp.exp(scores - jnp.max(scores, axis=1, keepdims=True))
    probs_full = probs_full / jnp.sum(probs_full, axis=1, keepdims=True)
    probs_low = probs_full.astype(jnp.bfloat16)
    attended = jnp.dot(probs_low, value_rows, preferred_element_type=jnp.float32).astype(jnp.bfloat16)
    grad_probs = jnp.dot(grad_rows, value_rows.T, preferred_element_type=jnp.float32)
    row_delta = jnp.sum(grad_rows.astype(jnp.float32) * attended.astype(jnp.float32), axis=1, keepdims=True)
    grad_scores = (probs_full * (grad_probs - row_delta)).astype(jnp.bfloat16)
    grad_query = att_scale * jnp.dot(grad_scores, key_rows, preferred_element_type=jnp.float32)
    grad_key = att_scale * jnp.dot(grad_scores.T, query_rows, preferred_element_type=jnp.float32)
    grad_value = jnp.dot(probs_low.T, grad_rows, preferred_element_type=jnp.float32)
    return attended, grad_query, grad_key, grad_value


def reference(output_gradient, expert_choice_index, routing_weight, stored_gate_preact, gate_up_weight, down_weight, down_first_factor, down_second_factor, rotated_queries, rotated_keys, stored_values, output_weight, output_first_factor, output_second_factor):
    block_count = TOKEN_TOTAL // TOK_DEV
    per_block = expert_choice_index.reshape(block_count, TOK_DEV * TOP)
    onehot = (per_block[:, :, None] == jnp.arange(EXPERT_COUNT, dtype=jnp.int32)[None, None, :]).astype(jnp.int32)
    before = jnp.cumsum(onehot, axis=1) - onehot
    slot_rank = jnp.sum(before * onehot, axis=2)
    source = jnp.arange(block_count, dtype=jnp.int32)[:, None]
    cells = (source * CAP + slot_rank).reshape(-1).astype(jnp.int32)
    gathered_owner = jnp.full((EXPERT_COUNT, SLOTS), -1, jnp.int32)
    gathered_owner = gathered_owner.at[expert_choice_index.reshape(-1), cells].set(jnp.arange(TOKEN_TOTAL * TOP, dtype=jnp.int32))
    flat_weights = routing_weight.reshape(-1)

    def expert_step(carry, packed):
        owners, saved_rows, gate_up, down_output, lowrank_first, low_b = packed
        live = owners >= 0
        safe_owner = jnp.maximum(owners, 0)
        token_rows = safe_owner // TOP
        weight = jnp.where(live, flat_weights[safe_owner], jnp.float32(0.0))
        routed_rows = (weight[:, None] * output_gradient[token_rows].astype(jnp.float32)).astype(jnp.bfloat16)
        grad_rows, gradient_first, gradient_second = expert_backward(routed_rows, saved_rows, gate_up, down_output, lowrank_first, low_b)
        contrib = jnp.where(live[:, None], grad_rows.astype(jnp.float32), jnp.float32(0.0))
        carry = carry.at[token_rows].add(contrib)
        return carry, (gradient_first, gradient_second)

    offset_prefix = jnp.zeros((TOKEN_TOTAL, MODEL_DIM), jnp.float32)
    merged_result, (first_factor_gradient, second_factor_gradient) = lax.scan(expert_step, offset_prefix, (gathered_owner, stored_gate_preact, gate_up_weight, down_weight, down_first_factor, down_second_factor))
    residual_gradient = (output_gradient.astype(jnp.float32) + merged_result).astype(jnp.bfloat16)

    lowrank_token = jnp.dot(residual_gradient, output_second_factor.T, preferred_element_type=jnp.float32).astype(jnp.bfloat16)
    head_gradient = (jnp.dot(residual_gradient, output_weight.T, preferred_element_type=jnp.float32) + adapter_scale * jnp.dot(lowrank_token, output_first_factor, preferred_element_type=jnp.float32)).astype(jnp.bfloat16)
    group_size = QUERY_HEADS // KVH

    def head_turn(number):
        piece_index = number // QUERY_HEADS
        head_index = number % QUERY_HEADS
        kv_index = head_index // group_size
        first_row = (piece_index * PIECE).astype(jnp.int32)
        query_rows = lax.dynamic_slice(rotated_queries, (first_row, (head_index * HEAD_SIZE).astype(jnp.int32)), (PIECE, HEAD_SIZE))
        grad_rows = lax.dynamic_slice(head_gradient, (first_row, (head_index * HEAD_SIZE).astype(jnp.int32)), (PIECE, HEAD_SIZE))
        key_rows = lax.dynamic_slice(rotated_keys, (first_row, (kv_index * HEAD_SIZE).astype(jnp.int32)), (PIECE, HEAD_SIZE))
        value_rows = lax.dynamic_slice(stored_values, (first_row, (kv_index * HEAD_SIZE).astype(jnp.int32)), (PIECE, HEAD_SIZE))
        return head_backward(query_rows, key_rows, value_rows, grad_rows)

    attended, grad_q, grad_k, grad_v = lax.map(head_turn, jnp.arange(N_GRP * QUERY_HEADS, dtype=jnp.int32))
    query_gradient = grad_q.reshape(N_GRP, QUERY_HEADS, PIECE, HEAD_SIZE).transpose(0, 2, 1, 3).reshape(TOKEN_TOTAL, QUERY_HEADS * HEAD_SIZE)
    key_gradient = grad_k.reshape(N_GRP, KVH, group_size, PIECE, HEAD_SIZE).sum(axis=2).transpose(0, 2, 1, 3).reshape(TOKEN_TOTAL, KVH * HEAD_SIZE)
    value_gradient = grad_v.reshape(N_GRP, KVH, group_size, PIECE, HEAD_SIZE).sum(axis=2).transpose(0, 2, 1, 3).reshape(TOKEN_TOTAL, KVH * HEAD_SIZE)
    attended_gathered = attended.reshape(N_GRP, QUERY_HEADS, PIECE, HEAD_SIZE).transpose(0, 2, 1, 3).reshape(TOKEN_TOTAL, QUERY_HEADS, HEAD_SIZE)
    output_first_gradient = adapter_scale * jnp.dot(lowrank_token.T, attended_gathered.reshape(TOKEN_TOTAL, QUERY_HEADS * HEAD_SIZE), preferred_element_type=jnp.float32)
    flattened = jnp.einsum('fxm,oxm->fxo', attended_gathered.astype(jnp.float32), output_first_factor.reshape(ADAPTER_RANK, QUERY_HEADS, HEAD_SIZE).astype(jnp.float32)).astype(jnp.bfloat16)
    output_second_gradient = adapter_scale * jnp.einsum('dfn,dj->nj', flattened.astype(jnp.float32), residual_gradient.astype(jnp.float32))
    return (first_factor_gradient, second_factor_gradient, residual_gradient, output_first_gradient, output_second_gradient, query_gradient, key_gradient, value_gradient)
```

```python
import functools

import jax
import jax.numpy as jnp
from jax import lax
from jax.experimental import pallas as pl
from jax.experimental.pallas import tpu as pltpu
from jax.sharding import PartitionSpec as P

QUERY_HEADS = 32
KVH = 4
HEAD_SIZE = 128
MESH = pl.DeviceIdType.MESH
ALL = ("grp", "dev")

adapter_scale = 2.0
neg_big = -1e30
f32 = jnp.float32
bf16 = jnp.bfloat16


def contraction(left, right, left_dim, right_dim):
    return lax.dot_general(
        left, right, (((left_dim,), (right_dim,)), ((), ())), preferred_element_type=f32
    )


def dispatch_kernel(capacity, x_ref, idx_ref, w_ref, out_ref, cells_ref, rows, tok_v, wt_v, tok_s, wt_s, sems):
    tokens, width = x_ref.shape
    sub = width // 128
    per_step = out_ref.shape[0] // capacity
    step = pl.program_id(0)

    @pl.when(step == 0)
    def _():
        for b in range(sub):
            rows[pl.ds(b, tokens, stride=sub), :] = x_ref[:, b * 128 : (b + 1) * 128].astype(f32)
        shape = (tokens, 128)
        t_iota = lax.broadcasted_iota(jnp.int32, shape, 0)
        e_iota = lax.broadcasted_iota(jnp.int32, shape, 1)
        idx = idx_ref[...]
        w = w_ref[...]
        named = jnp.zeros(shape, f32)
        weight = jnp.zeros(shape, f32)
        for k in range(idx.shape[1]):
            hit = idx[:, k : k + 1] == e_iota
            named = named + jnp.where(hit, 1.0, 0.0)
            weight = weight + jnp.where(hit, w[:, k : k + 1], 0.0)
        earlier = jnp.where(t_iota > e_iota, 1.0, 0.0).astype(bf16)
        rank = jnp.dot(earlier, named.astype(bf16), preferred_element_type=f32)
        t_float = t_iota.astype(f32)
        for c in range(capacity):
            mine = jnp.logical_and(named > 0.5, rank == float(c))
            tok_v[c : c + 1, :] = jnp.sum(
                jnp.where(mine, t_float, 0.0), axis=0, keepdims=True
            ).astype(jnp.int32)
            wt_v[c : c + 1, :] = jnp.sum(jnp.where(mine, weight, 0.0), axis=0, keepdims=True)
        cells = jnp.zeros(shape, f32)
        for k in range(idx.shape[1]):
            hit = idx[:, k : k + 1] == e_iota
            place = jnp.sum(jnp.where(hit, rank, 0.0), axis=1, keepdims=True)
            place = place + float(capacity) * idx[:, k : k + 1].astype(f32)
            cells = cells + jnp.where(e_iota == k, place, 0.0)
        cells_ref[...] = cells.astype(jnp.int32)
        one = pltpu.make_async_copy(tok_v, tok_s, sems.at[0])
        two = pltpu.make_async_copy(wt_v, wt_s, sems.at[1])
        one.start()
        two.start()
        one.wait()
        two.wait()

    def expert(j, carry):
        e = step * per_step + j
        for c in range(capacity):
            start = pl.multiple_of(tok_s[c, e] * sub, sub)
            out_ref[j * capacity + c] = (rows[pl.ds(start, sub), :] * wt_s[c, e]).astype(bf16)
        return carry

    lax.fori_loop(0, per_step, expert, 0, unroll=2)


def dispatch(x, idx, w, experts, capacity):
    tokens, width = x.shape
    sub = width // 128
    steps = 8
    slots = experts * capacity
    pad = -(-capacity // 8) * 8
    return pl.pallas_call(
        functools.partial(dispatch_kernel, capacity),
        grid=(steps,),
        out_shape=(
            jax.ShapeDtypeStruct((slots, sub, 128), bf16),
            jax.ShapeDtypeStruct((tokens, 128), jnp.int32),
        ),
        in_specs=[
            pl.BlockSpec((tokens, width), lambda i: (0, 0)),
            pl.BlockSpec(idx.shape, lambda i: (0, 0)),
            pl.BlockSpec(w.shape, lambda i: (0, 0)),
        ],
        out_specs=(
            pl.BlockSpec((slots // steps, sub, 128), lambda i: (i, 0, 0)),
            pl.BlockSpec((tokens, 128), lambda i: (0, 0)),
        ),
        scratch_shapes=[
            pltpu.VMEM((tokens * sub, 128), f32),
            pltpu.VMEM((pad, 128), jnp.int32),
            pltpu.VMEM((pad, 128), f32),
            pltpu.SMEM((pad, 128), jnp.int32),
            pltpu.SMEM((pad, 128), f32),
            pltpu.SemaphoreType.DMA((2,)),
        ],
        compiler_params=pltpu.CompilerParams(dimension_semantics=("arbitrary",)),
        name="dispatch",
    )(x, idx, w)


def expert_kernel(r_ref, s_ref, g_ref, d_ref, a_ref, b_ref, out_ref, first_ref, second_ref, wide, rows):
    count, sub, _ = r_ref.shape
    ff = d_ref.shape[0]

    @pl.when(pl.program_id(0) == 0)
    def _():
        first_ref[...] = jnp.zeros_like(first_ref)
        second_ref[...] = jnp.zeros_like(second_ref)

    wide[...] = r_ref[...].astype(f32).reshape(count * sub, 128)
    for b in range(sub):
        rows[:, b * 128 : (b + 1) * 128] = wide[pl.ds(b, count, stride=sub), :].astype(bf16)
    x = rows[...]
    pre_gate = s_ref[:, :ff].astype(f32)
    pre_up = s_ref[:, ff:].astype(f32)
    sigmoid = jax.nn.sigmoid(pre_gate)
    activated = pre_gate * sigmoid
    slope = sigmoid * (1.0 + pre_gate * (1.0 - sigmoid))
    hidden = (activated * pre_up).astype(bf16)
    low_in = contraction(hidden, a_ref[...], 1, 1).astype(bf16)
    low_grad = contraction(x, b_ref[...], 1, 1).astype(bf16)
    second_ref[...] += adapter_scale * contraction(low_in, x, 0, 0)
    first_ref[...] += adapter_scale * contraction(low_grad, hidden, 0, 0)
    grad_hidden = contraction(x, d_ref[...], 1, 1) + adapter_scale * jnp.dot(
        low_grad, a_ref[...], preferred_element_type=f32
    )
    left = (grad_hidden * (pre_up * slope)).astype(bf16)
    right = (grad_hidden * activated).astype(bf16)
    for b in range(0, sub, 2):
        at = slice(b * 128, (b + 2) * 128)
        res = contraction(left, g_ref[at, :ff], 1, 1) + contraction(right, g_ref[at, ff:], 1, 1)
        wide[pl.ds(b, count, stride=sub), :] = res[:, :128]
        wide[pl.ds(b + 1, count, stride=sub), :] = res[:, 128:]
    out_ref[...] = wide[...].reshape(count, sub, 128).astype(bf16)


def experts_backward(routed, saved, gate_up, down, first, second, count):
    slots, sub, _ = routed.shape
    ff, width = down.shape
    rank = first.shape[0]
    once = pl.Buffered(1)
    whole = lambda shape: pl.BlockSpec(shape, lambda i: (0, 0), pipeline_mode=once)
    return pl.pallas_call(
        expert_kernel,
        grid=(slots // count,),
        out_shape=(
            jax.ShapeDtypeStruct((slots, sub, 128), bf16),
            jax.ShapeDtypeStruct((rank, ff), f32),
            jax.ShapeDtypeStruct((rank, width), f32),
        ),
        in_specs=[
            pl.BlockSpec((count, sub, 128), lambda i: (i, 0, 0)),
            pl.BlockSpec((count, 2 * ff), lambda i: (i, 0)),
            whole(gate_up.shape),
            whole(down.shape),
            whole(first.shape),
            whole(second.shape),
        ],
        out_specs=(
            pl.BlockSpec((count, sub, 128), lambda i: (i, 0, 0)),
            pl.BlockSpec((rank, ff), lambda i: (0, 0)),
            pl.BlockSpec((rank, width), lambda i: (0, 0)),
        ),
        scratch_shapes=[pltpu.VMEM((count * sub, 128), f32), pltpu.VMEM((count, width), bf16)],
        compiler_params=pltpu.CompilerParams(
            dimension_semantics=("arbitrary",), vmem_limit_bytes=56 << 20
        ),
        cost_estimate=pl.CostEstimate(flops=13_500_000_000, bytes_accessed=24_000_000, transcendentals=0),
        name="experts",
    )(routed, saved, gate_up, down, first, second)


def combine_kernel(cells_ref, x_ref, r_ref, out_ref, rows):
    tokens, width = x_ref.shape
    sub = width // 128
    top = cells_ref.shape[1]

    def token(t, carry):
        total = r_ref[cells_ref[t, 0]].astype(f32)
        for k in range(1, top):
            total = total + r_ref[cells_ref[t, k]].astype(f32)
        rows[pl.ds(pl.multiple_of(t * sub, sub), sub), :] = total
        return carry

    lax.fori_loop(0, tokens, token, 0, unroll=4)
    for b in range(sub):
        at = slice(b * 128, (b + 1) * 128)
        out_ref[:, at] = (
            x_ref[:, at].astype(f32) + rows[pl.ds(b, tokens, stride=sub), :]
        ).astype(bf16)


def combine(cells, x, returned):
    tokens, width = x.shape
    return pl.pallas_call(
        combine_kernel,
        out_shape=jax.ShapeDtypeStruct(x.shape, bf16),
        in_specs=[
            pl.BlockSpec(memory_space=pltpu.SMEM),
            pl.BlockSpec(memory_space=pltpu.VMEM),
            pl.BlockSpec(memory_space=pltpu.VMEM),
        ],
        out_specs=pl.BlockSpec(memory_space=pltpu.VMEM),
        scratch_shapes=[pltpu.VMEM((tokens * width // 128, 128), f32)],
        name="combine",
    )(cells, x, returned)


def gather_kernel(x_ref, y_ref, spare, us, ds, xs, cs, ur, dr, xr, cr, lsem):
    g = lax.axis_index("grp")
    d = lax.axis_index("dev")
    y = d // 4
    xl = (d // 2) % 2
    c = d % 2
    half = x_ref.shape[0] // 2

    def idx(yy, xx):
        return yy * 4 + xx * 2 + c

    px = 1 - xl
    up, dn, op = (y + 1) % 4, (y + 3) % 4, (y + 2) % 4
    to_up, to_dn, to_x = (g, idx(up, xl)), (g, idx(dn, xl)), (g, idx(y, px))
    to_c = (g, y * 4 + xl * 2 + (1 - c))
    barrier = pltpu.get_barrier_semaphore()
    for target in (to_up, to_dn, to_x, to_c):
        pl.semaphore_signal(barrier, inc=1, device_id=target, device_id_type=MESH)
    pl.semaphore_wait(barrier, 4)
    A, B = 0, 1

    def part(h):
        return x_ref.at[pl.ds(h * half, half)]

    def at(o, h):
        return y_ref.at[o, pl.ds(h * half, half)]

    mine = idx(y, xl)
    sends = []
    order = []

    def send(src, o, h, target, ssem, rsem):
        copy = pltpu.make_async_remote_copy(
            src_ref=src, dst_ref=at(o, h), send_sem=ssem, recv_sem=rsem,
            device_id=target, device_id_type=MESH,
        )
        copy.start()
        sends.append(copy)

    def arrived(o, h, sem):
        pltpu.make_async_remote_copy(
            src_ref=at(o, h), dst_ref=at(o, h), send_sem=spare, recv_sem=sem,
            device_id=to_c, device_id_type=MESH,
        ).wait_recv()

    def across(src, o, h):
        i = len(order)
        order.append((o, h))
        send(src, o, h, to_c, cs.at[i], cr.at[i])

    own = pltpu.make_async_copy(x_ref, y_ref.at[mine], lsem)
    own.start()
    send(part(A), mine, A, to_dn, ds.at[0], ur.at[0])
    send(part(B), mine, B, to_up, us.at[0], dr.at[0])
    send(part(A), mine, A, to_x, xs.at[0], xr.at[0])
    send(part(B), mine, B, to_dn, ds.at[1], ur.at[1])
    send(part(A), mine, A, to_up, us.at[1], dr.at[1])
    send(part(B), mine, B, to_x, xs.at[1], xr.at[1])
    across(part(A), mine, A)
    across(part(B), mine, B)
    steps = (
        (up, xl, A, ur, 0, to_dn, ds, ur, 2),
        (dn, xl, B, dr, 0, to_up, us, dr, 2),
        (y, px, A, xr, 0, to_dn, ds, ur, 3),
        (up, xl, B, ur, 1, to_x, xs, xr, 2),
        (dn, xl, A, dr, 1, to_x, xs, xr, 3),
        (y, px, B, xr, 1, to_up, us, dr, 3),
        (op, xl, A, ur, 2, None, None, None, 0),
        (op, xl, B, dr, 2, None, None, None, 0),
        (up, px, A, ur, 3, to_dn, ds, ur, 4),
        (dn, px, B, dr, 3, to_up, us, dr, 4),
        (up, px, B, xr, 2, None, None, None, 0),
        (dn, px, A, xr, 3, None, None, None, 0),
        (op, px, A, ur, 4, None, None, None, 0),
        (op, px, B, dr, 4, None, None, None, 0),
    )
    for yy, xx, h, sems, i, target, ssems, rsems, j in steps:
        o = idx(yy, xx)
        arrived(o, h, sems.at[i])
        if target is not None:
            send(at(o, h), o, h, target, ssems.at[j], rsems.at[j])
        across(at(o, h), o, h)
    for i, (o, h) in enumerate(order):
        arrived(o + 1 - 2 * c, h, cr.at[i])
    for copy in sends:
        copy.wait_send()
    own.wait()


def gather_piece(x, members):
    sem = pltpu.SemaphoreType.DMA
    return pl.pallas_call(
        gather_kernel,
        out_shape=jax.ShapeDtypeStruct((members,) + x.shape, x.dtype),
        in_specs=[pl.BlockSpec(memory_space=pl.ANY)],
        out_specs=pl.BlockSpec(memory_space=pl.ANY),
        scratch_shapes=[
            sem, sem((5,)), sem((5,)), sem((4,)), sem((16,)),
            sem((5,)), sem((5,)), sem((4,)), sem((16,)), sem,
        ],
        compiler_params=pltpu.CompilerParams(collective_id=1, has_side_effects=True),
        name="gather_piece",
    )(x)


BLOCK = 512


def forward_kernel(kv_ref, q_ref, k_ref, v_ref, probs_ref, att_ref, scores, value_t):
    block = q_ref.shape[0]
    scale = HEAD_SIZE ** (-0.5)
    number = pl.program_id(1)

    @pl.when(jnp.logical_and(pl.program_id(0) == 0, number == 0))
    def _():
        value_t[...] = v_ref[...].astype(f32).T.astype(bf16)

    q = q_ref[...]
    above = lax.broadcasted_iota(jnp.int32, (block, block), 0) > lax.broadcasted_iota(
        jnp.int32, (block, block), 1
    )

    def rows(j):
        return pl.ds(pl.multiple_of(j * block, block), block)

    def score(j):
        return contraction(k_ref[rows(j), :], q, 1, 1) * scale

    def one(j, top):
        s = score(j)
        scores[rows(j), :] = s
        return jnp.maximum(top, jnp.max(s, axis=0, keepdims=True))

    s = jnp.where(above, neg_big, score(number))
    scores[rows(number), :] = s
    top = lax.fori_loop(0, number, one, jnp.max(s, axis=0, keepdims=True))

    def two(j, total):
        e = jnp.exp(scores[rows(j), :] - top)
        scores[rows(j), :] = e
        return total + jnp.sum(e, axis=0, keepdims=True)

    total = lax.fori_loop(0, number + 1, two, jnp.zeros((1, block), f32))
    share = 1.0 / total

    def three(j, acc):
        p = (scores[rows(j), :] * share).astype(bf16)
        probs_ref[0, 0, rows(j), :] = p
        return acc + jnp.dot(value_t[:, rows(j)], p, preferred_element_type=f32)

    acc = lax.fori_loop(0, number + 1, three, jnp.zeros((HEAD_SIZE, block), f32))
    att_ref[...] = acc.T.astype(bf16)


def attention_forward(kv_index, queries, keys, values):
    piece, cols = queries.shape
    heads = cols // HEAD_SIZE
    blocks = piece // BLOCK
    grid_spec = pltpu.PrefetchScalarGridSpec(
        num_scalar_prefetch=1,
        grid=(heads, blocks),
        in_specs=[
            pl.BlockSpec((BLOCK, HEAD_SIZE), lambda h, i, kv: (i, h)),
            pl.BlockSpec((piece, HEAD_SIZE), lambda h, i, kv: (0, kv[0])),
            pl.BlockSpec((piece, HEAD_SIZE), lambda h, i, kv: (0, kv[0])),
        ],
        out_specs=(
            pl.BlockSpec((1, 1, piece, BLOCK), lambda h, i, kv: (h, i, 0, 0)),
            pl.BlockSpec((BLOCK, HEAD_SIZE), lambda h, i, kv: (i, h)),
        ),
        scratch_shapes=[pltpu.VMEM((piece, BLOCK), f32), pltpu.VMEM((HEAD_SIZE, piece), bf16)],
    )
    return pl.pallas_call(
        forward_kernel,
        grid_spec=grid_spec,
        out_shape=(
            jax.ShapeDtypeStruct((heads, blocks, piece, BLOCK), bf16),
            jax.ShapeDtypeStruct((piece, cols), bf16),
        ),
        compiler_params=pltpu.CompilerParams(
            dimension_semantics=("arbitrary", "arbitrary"), vmem_limit_bytes=40 << 20
        ),
        cost_estimate=pl.CostEstimate(
            flops=20_000_000_000, bytes_accessed=40_000_000, transcendentals=5_000_000
        ),
        name="attention_forward",
    )(kv_index, queries, keys, values)


def backward_kernel(kv_ref, p_ref, q_ref, g_ref, att_ref, k_ref, v_ref, dq_ref, kv_out, key_t, key_sum, value_sum):
    block = q_ref.shape[0]
    scale = HEAD_SIZE ** (-0.5)
    head, number = pl.program_id(0), pl.program_id(1)

    @pl.when(jnp.logical_and(head == 0, number == 0))
    def _():
        key_t[...] = k_ref[...].astype(f32).T.astype(bf16)
        key_sum[...] = jnp.zeros_like(key_sum)
        value_sum[...] = jnp.zeros_like(value_sum)

    q = q_ref[...]
    g = g_ref[...]
    delta = jnp.sum((g.astype(f32) * att_ref[...].astype(f32)).T, axis=0, keepdims=True)

    def rows(j):
        return pl.ds(pl.multiple_of(j * block, block), block)

    def turn(j, acc):
        p = p_ref[0, 0, rows(j), :]
        grad = contraction(v_ref[rows(j), :], g, 1, 1)
        ds = (p.astype(f32) * (grad - delta)).astype(bf16)
        value_sum[rows(j), :] += jnp.dot(p, g, preferred_element_type=f32)
        key_sum[rows(j), :] += jnp.dot(ds, q, preferred_element_type=f32)
        return acc + jnp.dot(key_t[:, rows(j)], ds, preferred_element_type=f32)

    acc = lax.fori_loop(0, number + 1, turn, jnp.zeros((HEAD_SIZE, block), f32))
    dq_ref[...] = acc.T * scale

    @pl.when(jnp.logical_and(head == pl.num_programs(0) - 1, number == pl.num_programs(1) - 1))
    def _():
        kv_out[:, :HEAD_SIZE] = (key_sum[...] * scale).astype(bf16)
        kv_out[:, HEAD_SIZE:] = value_sum[...].astype(bf16)


def attention_backward(kv_index, probs, queries, grads, attended, keys, values):
    piece, cols = queries.shape
    heads = cols // HEAD_SIZE
    blocks = piece // BLOCK
    tile = pl.BlockSpec((BLOCK, HEAD_SIZE), lambda h, i, kv: (i, h))
    column = pl.BlockSpec((piece, HEAD_SIZE), lambda h, i, kv: (0, kv[0]))
    grid_spec = pltpu.PrefetchScalarGridSpec(
        num_scalar_prefetch=1,
        grid=(heads, blocks),
        in_specs=[
            pl.BlockSpec((1, 1, piece, BLOCK), lambda h, i, kv: (h, i, 0, 0)),
            tile,
            tile,
            tile,
            column,
            column,
        ],
        out_specs=(tile, pl.BlockSpec((piece, 2 * HEAD_SIZE), lambda h, i, kv: (0, 0))),
        scratch_shapes=[
            pltpu.VMEM((HEAD_SIZE, piece), bf16),
            pltpu.VMEM((piece, HEAD_SIZE), f32),
            pltpu.VMEM((piece, HEAD_SIZE), f32),
        ],
    )
    return pl.pallas_call(
        backward_kernel,
        grid_spec=grid_spec,
        out_shape=(
            jax.ShapeDtypeStruct((piece, cols), f32),
            jax.ShapeDtypeStruct((piece, 2 * HEAD_SIZE), bf16),
        ),
        compiler_params=pltpu.CompilerParams(
            dimension_semantics=("arbitrary", "arbitrary"), vmem_limit_bytes=40 << 20
        ),
        cost_estimate=pl.CostEstimate(
            flops=20_000_000_000, bytes_accessed=30_000_000, transcendentals=0
        ),
        name="attention_backward",
    )(kv_index, probs, queries, grads, attended, keys, values)


def exchange(x, axes):
    return lax.all_to_all(x, axes, split_axis=0, concat_axis=0, tiled=True)


def on_device(
    output_gradient,
    expert_choice_index,
    routing_weight,
    stored_gate_preact,
    gate_up_weight,
    down_weight,
    down_first_factor,
    down_second_factor,
    rotated_queries,
    rotated_keys,
    stored_values,
    output_weight,
    output_first_factor,
    output_second_factor,
):
    tok_rows, model_width = output_gradient.shape
    grp_count = lax.axis_size("grp")
    dev_count = lax.axis_size("dev")
    experts = grp_count * dev_count
    slot_count = stored_gate_preact.shape[1]
    capacity = slot_count // experts
    sub = model_width // 128
    piece_len, share_cols = rotated_queries.shape
    device_share = share_cols // HEAD_SIZE
    group_size = QUERY_HEADS // KVH
    rank_total = output_second_factor.shape[0]
    kv_index = (lax.axis_index("dev") * device_share // group_size).astype(jnp.int32).reshape(1)

    outgoing, cells = dispatch(
        output_gradient, expert_choice_index, routing_weight, experts, capacity
    )
    incoming = exchange(outgoing.reshape(experts, capacity, sub, 128), ALL)
    probs, attended = attention_forward(kv_index, rotated_queries, rotated_keys, stored_values)
    spread = jnp.zeros((device_share, rank_total, device_share, HEAD_SIZE), bf16)
    for h in range(device_share):
        spread = spread.at[h, :, h, :].set(
            output_first_factor[:, h * HEAD_SIZE : (h + 1) * HEAD_SIZE]
        )
    spread = spread.reshape(device_share * rank_total, share_cols)
    folded = contraction(attended, spread, 1, 1).astype(bf16)

    grad_rows, gradient_first, gradient_second = experts_backward(
        incoming.reshape(slot_count, sub, 128),
        stored_gate_preact[0],
        gate_up_weight[0],
        down_weight[0],
        down_first_factor[0],
        down_second_factor[0],
        256,
    )
    returned = exchange(grad_rows.reshape(experts, capacity, sub, 128), ALL)
    residual_gradient = combine(
        cells[:, : expert_choice_index.shape[1]],
        output_gradient,
        returned.reshape(slot_count, sub, 128),
    )
    segment_gradient = gather_piece(residual_gradient, dev_count).reshape(piece_len, model_width)

    lowrank_token = contraction(segment_gradient, output_second_factor, 1, 1).astype(bf16)
    head_gradient = (
        contraction(segment_gradient, output_weight, 1, 1)
        + adapter_scale * jnp.dot(lowrank_token, output_first_factor, preferred_element_type=f32)
    ).astype(bf16)
    row_contrib = (adapter_scale * contraction(lowrank_token, attended, 0, 0)).astype(bf16)
    column_contrib = contraction(folded, segment_gradient, 0, 0)
    column_contrib = adapter_scale * jnp.sum(
        column_contrib.reshape(device_share, rank_total, model_width), axis=0
    )

    tiles = column_contrib.reshape(rank_total // 8, 8, model_width // 128, 128)
    tiles = tiles.transpose(0, 2, 1, 3).reshape(experts, 8, 128)
    tile = jnp.sum(exchange(tiles, ALL), axis=0)
    tiles = exchange(jnp.broadcast_to(tile[None], (experts, 8, 128)), ALL)
    tiles = tiles.reshape(rank_total // 8, model_width // 128, 8, 128).transpose(0, 2, 1, 3)
    output_second_gradient = tiles.reshape(rank_total, model_width)
    row_all = exchange(jnp.broadcast_to(row_contrib[None], (grp_count,) + row_contrib.shape), "grp")
    output_first_gradient = jnp.sum(row_all.astype(f32), axis=0)

    query_gradient, kv_terms = attention_backward(
        kv_index, probs, rotated_queries, head_gradient, attended, rotated_keys, stored_values
    )
    kv_all = exchange(kv_terms.reshape(dev_count, tok_rows, 2 * HEAD_SIZE), "dev")
    kv_sum = jnp.sum(
        kv_all.reshape(KVH, dev_count // KVH, tok_rows, 2 * HEAD_SIZE).astype(f32), axis=1
    )
    key_gradient = kv_sum[:, :, :HEAD_SIZE].transpose(1, 0, 2).reshape(tok_rows, KVH * HEAD_SIZE)
    value_gradient = kv_sum[:, :, HEAD_SIZE:].transpose(1, 0, 2).reshape(tok_rows, KVH * HEAD_SIZE)
    return (
        gradient_first[None],
        gradient_second[None],
        residual_gradient,
        output_first_gradient,
        output_second_gradient,
        query_gradient,
        key_gradient,
        value_gradient,
    )


def solution(mesh):
    in_specs = (
        P(("grp", "dev"), None),
        P(("grp", "dev"), None),
        P(("grp", "dev"), None),
        P(("grp", "dev"), None, None),
        P(("grp", "dev"), None, None),
        P(("grp", "dev"), None, None),
        P(("grp", "dev"), None, None),
        P(("grp", "dev"), None, None),
        P("grp", "dev"),
        P("grp", None),
        P("grp", None),
        P("dev", None),
        P(None, "dev"),
        P(),
    )
    out_specs = (
        P(("grp", "dev"), None, None),
        P(("grp", "dev"), None, None),
        P(("grp", "dev"), None),
        P(None, "dev"),
        P(),
        P("grp", "dev"),
        P(("grp", "dev"), None),
        P(("grp", "dev"), None),
    )
    return jax.shard_map(
        on_device, mesh=mesh, in_specs=in_specs, out_specs=out_specs, check_vma=False
    )
```

```python
import functools

import jax
import jax.numpy as jnp
from jax import lax
from jax.experimental import pallas as pl
from jax.experimental.pallas import tpu as pltpu
from jax.sharding import PartitionSpec as P

QUERY_HEADS = 32
KVH = 4
HEAD_SIZE = 128
MESH = pl.DeviceIdType.MESH
ALL = ("grp", "dev")

adapter_scale = 2.0
neg_big = -1e30
f32 = jnp.float32
bf16 = jnp.bfloat16


def contraction(left, right, left_dim, right_dim):
    return lax.dot_general(
        left, right, (((left_dim,), (right_dim,)), ((), ())), preferred_element_type=f32
    )


def dispatch_kernel(capacity, x_ref, idx_ref, w_ref, out_ref, cells_ref, rows, tok_v, wt_v, tok_s, wt_s, sems):
    tokens, width = x_ref.shape
    sub = width // 128
    per_step = out_ref.shape[0] // capacity
    step = pl.program_id(0)

    @pl.when(step == 0)
    def _():
        for b in range(sub):
            rows[pl.ds(b, tokens, stride=sub), :] = x_ref[:, b * 128 : (b + 1) * 128].astype(f32)
        shape = tok_v.shape
        e_iota = lax.broadcasted_iota(jnp.int32, shape, 0)
        t_iota = lax.broadcasted_iota(jnp.int32, shape, 1)
        idx = idx_ref[...]
        w = w_ref[...]
        named = jnp.zeros(shape, f32)
        weight = jnp.zeros(shape, f32)
        for k in range(idx.shape[0]):
            hit = idx[k : k + 1, :] == e_iota
            named = named + jnp.where(hit, 1.0, 0.0)
            weight = weight + jnp.where(hit, w[k : k + 1, :], 0.0)
        earlier = jnp.where(e_iota < t_iota, 1.0, 0.0).astype(bf16)
        rank = jnp.dot(named.astype(bf16), earlier, preferred_element_type=f32)
        t_float = t_iota.astype(f32)
        toks = jnp.zeros(shape, f32)
        wts = jnp.zeros(shape, f32)
        for c in range(capacity):
            mine = jnp.logical_and(named > 0.5, rank == float(c))
            tok = jnp.sum(jnp.where(mine, t_float, 0.0), axis=1, keepdims=True)
            wt = jnp.sum(jnp.where(mine, weight, 0.0), axis=1, keepdims=True)
            toks = jnp.where(t_iota == c, tok, toks)
            wts = jnp.where(t_iota == c, wt, wts)
        tok_v[...] = toks.astype(jnp.int32)
        wt_v[...] = wts
        for k in range(idx.shape[0]):
            hit = idx[k : k + 1, :] == e_iota
            place = jnp.sum(jnp.where(hit, rank, 0.0), axis=0, keepdims=True)
            cells_ref[k : k + 1, :] = place.astype(jnp.int32) + capacity * idx[k : k + 1, :]
        one = pltpu.make_async_copy(tok_v, tok_s, sems.at[0])
        two = pltpu.make_async_copy(wt_v, wt_s, sems.at[1])
        one.start()
        two.start()
        one.wait()
        two.wait()

    def expert(j, carry):
        e = step * per_step + j
        for c in range(capacity):
            start = pl.multiple_of(tok_s[e, c] * sub, sub)
            out_ref[j * capacity + c] = (rows[pl.ds(start, sub), :] * wt_s[e, c]).astype(bf16)
        return carry

    lax.fori_loop(0, per_step, expert, 0, unroll=2)


def dispatch(x, idx, w, experts, capacity):
    tokens, width = x.shape
    sub = width // 128
    steps = 8
    slots = experts * capacity
    idx, w = idx.T, w.T
    return pl.pallas_call(
        functools.partial(dispatch_kernel, capacity),
        grid=(steps,),
        out_shape=(
            jax.ShapeDtypeStruct((slots, sub, 128), bf16),
            jax.ShapeDtypeStruct(idx.shape, jnp.int32),
        ),
        in_specs=[
            pl.BlockSpec((tokens, width), lambda i: (0, 0)),
            pl.BlockSpec(idx.shape, lambda i: (0, 0)),
            pl.BlockSpec(w.shape, lambda i: (0, 0)),
        ],
        out_specs=(
            pl.BlockSpec((slots // steps, sub, 128), lambda i: (i, 0, 0)),
            pl.BlockSpec(idx.shape, lambda i: (0, 0)),
        ),
        scratch_shapes=[
            pltpu.VMEM((tokens * sub, 128), f32),
            pltpu.VMEM((experts, tokens), jnp.int32),
            pltpu.VMEM((experts, tokens), f32),
            pltpu.SMEM((experts, tokens), jnp.int32),
            pltpu.SMEM((experts, tokens), f32),
            pltpu.SemaphoreType.DMA((2,)),
        ],
        compiler_params=pltpu.CompilerParams(dimension_semantics=("arbitrary",)),
        name="dispatch",
    )(x, idx, w)


def expert_kernel(r_ref, s_ref, g_ref, d_ref, a_ref, b_ref, out_ref, first_ref, second_ref, wide, rows):
    count, sub, _ = r_ref.shape
    ff = d_ref.shape[0]

    @pl.when(pl.program_id(0) == 0)
    def _():
        first_ref[...] = jnp.zeros_like(first_ref)
        second_ref[...] = jnp.zeros_like(second_ref)

    wide[...] = r_ref[...].astype(f32).reshape(count * sub, 128)
    for b in range(sub):
        rows[:, b * 128 : (b + 1) * 128] = wide[pl.ds(b, count, stride=sub), :].astype(bf16)
    x = rows[...]
    pre_gate = s_ref[:, :ff].astype(f32)
    pre_up = s_ref[:, ff:].astype(f32)
    sigmoid = jax.nn.sigmoid(pre_gate)
    activated = pre_gate * sigmoid
    slope = sigmoid * (1.0 + pre_gate * (1.0 - sigmoid))
    hidden = (activated * pre_up).astype(bf16)
    low_in = contraction(hidden, a_ref[...], 1, 1).astype(bf16)
    low_grad = contraction(x, b_ref[...], 1, 1).astype(bf16)
    second_ref[...] += adapter_scale * contraction(low_in, x, 0, 0)
    first_ref[...] += adapter_scale * contraction(low_grad, hidden, 0, 0)
    grad_hidden = contraction(x, d_ref[...], 1, 1) + adapter_scale * jnp.dot(
        low_grad, a_ref[...], preferred_element_type=f32
    )
    left = (grad_hidden * (pre_up * slope)).astype(bf16)
    right = (grad_hidden * activated).astype(bf16)
    for b in range(0, sub, 2):
        at = slice(b * 128, (b + 2) * 128)
        res = contraction(left, g_ref[at, :ff], 1, 1) + contraction(right, g_ref[at, ff:], 1, 1)
        wide[pl.ds(b, count, stride=sub), :] = res[:, :128]
        wide[pl.ds(b + 1, count, stride=sub), :] = res[:, 128:]
    out_ref[...] = wide[...].reshape(count, sub, 128).astype(bf16)


def experts_backward(routed, saved, gate_up, down, first, second, count):
    slots, sub, _ = routed.shape
    ff, width = down.shape
    rank = first.shape[0]
    once = pl.Buffered(1)
    whole = lambda shape: pl.BlockSpec(shape, lambda i: (0, 0), pipeline_mode=once)
    return pl.pallas_call(
        expert_kernel,
        grid=(slots // count,),
        out_shape=(
            jax.ShapeDtypeStruct((slots, sub, 128), bf16),
            jax.ShapeDtypeStruct((rank, ff), f32),
            jax.ShapeDtypeStruct((rank, width), f32),
        ),
        in_specs=[
            pl.BlockSpec((count, sub, 128), lambda i: (i, 0, 0)),
            pl.BlockSpec((count, 2 * ff), lambda i: (i, 0)),
            whole(gate_up.shape),
            whole(down.shape),
            whole(first.shape),
            whole(second.shape),
        ],
        out_specs=(
            pl.BlockSpec((count, sub, 128), lambda i: (i, 0, 0)),
            pl.BlockSpec((rank, ff), lambda i: (0, 0)),
            pl.BlockSpec((rank, width), lambda i: (0, 0)),
        ),
        scratch_shapes=[pltpu.VMEM((count * sub, 128), f32), pltpu.VMEM((count, width), bf16)],
        compiler_params=pltpu.CompilerParams(
            dimension_semantics=("arbitrary",), vmem_limit_bytes=56 << 20
        ),
        cost_estimate=pl.CostEstimate(flops=13_500_000_000, bytes_accessed=24_000_000, transcendentals=0),
        name="experts",
    )(routed, saved, gate_up, down, first, second)


def combine_kernel(cells_ref, x_ref, r_ref, s_ref, out_ref, col_ref, rows):
    tokens, width = x_ref.shape
    sub = width // 128
    top = cells_ref.shape[0]

    def token(t, carry):
        total = r_ref[cells_ref[0, t]].astype(f32)
        for k in range(1, top):
            total = total + r_ref[cells_ref[k, t]].astype(f32)
        rows[pl.ds(pl.multiple_of(t * sub, sub), sub), :] = total
        return carry

    lax.fori_loop(0, tokens, token, 0, unroll=4)
    share = s_ref[...]
    high = share.astype(bf16)
    low = (share - high.astype(f32)).astype(bf16)
    for b in range(sub):
        at = slice(b * 128, (b + 1) * 128)
        res = (x_ref[:, at].astype(f32) + rows[pl.ds(b, tokens, stride=sub), :]).astype(bf16)
        out_ref[:, at] = res
        col_ref[:, at] = adapter_scale * (
            jnp.dot(high, res, preferred_element_type=f32)
            + jnp.dot(low, res, preferred_element_type=f32)
        )


def combine(cells, x, returned, share):
    tokens, width = x.shape
    vmem = pl.BlockSpec(memory_space=pltpu.VMEM)
    return pl.pallas_call(
        combine_kernel,
        out_shape=(
            jax.ShapeDtypeStruct(x.shape, bf16),
            jax.ShapeDtypeStruct((share.shape[0], width), f32),
        ),
        in_specs=[pl.BlockSpec(memory_space=pltpu.SMEM), vmem, vmem, vmem],
        out_specs=(vmem, vmem),
        scratch_shapes=[pltpu.VMEM((tokens * width // 128, 128), f32)],
        name="combine",
    )(cells, x, returned, share)


def remote(src, dst, ssem, rsem, target):
    return pltpu.make_async_remote_copy(
        src_ref=src, dst_ref=dst, send_sem=ssem, recv_sem=rsem,
        device_id=target, device_id_type=MESH,
    )


def greet(targets):
    barrier = pltpu.get_barrier_semaphore()
    for target in targets:
        pl.semaphore_signal(barrier, inc=1, device_id=target, device_id_type=MESH)
    pl.semaphore_wait(barrier, len(targets))


def share_kernel(devs, s_ref, out_ref, box, ssem, rsem, lsem):
    g = lax.axis_index("grp")
    d = lax.axis_index("dev")
    peers = [(g, (d + i) % devs) for i in range(1, devs)]
    greet(peers)

    def block(i):
        return s_ref.at[:, pl.ds(pl.multiple_of(i * 128, 128), 128)]

    for peer in peers:
        remote(block(peer[1]), box.at[d], ssem, rsem, peer).start()
    own = pltpu.make_async_copy(block(d), box.at[d], lsem)
    own.start()
    own.wait()
    part = box.at[pl.ds(0, devs - 1)]
    both = remote(part, part, ssem, rsem, peers[0])
    both.wait_send()
    both.wait_recv()
    total = box[0]
    for i in range(1, devs):
        total = total + box[i]
    out_ref[...] = total


def share_tokens(folded, devs):
    rank, piece = folded.shape
    sem = pltpu.SemaphoreType.DMA
    vmem = pl.BlockSpec(memory_space=pltpu.VMEM)
    return pl.pallas_call(
        functools.partial(share_kernel, devs),
        out_shape=jax.ShapeDtypeStruct((rank, piece // devs), f32),
        in_specs=[vmem],
        out_specs=vmem,
        scratch_shapes=[pltpu.VMEM((devs, rank, piece // devs), f32), sem, sem, sem],
        compiler_params=pltpu.CompilerParams(collective_id=2, has_side_effects=True),
        name="share_tokens",
    )(folded)


def gather_kernel(
    grps, devs, x_ref, col_ref, y_ref, tot_ref,
    spare, us, ds, xs, cs, ur, dr, xr, cr, lsem,
    box1, part, box2, tile, full, s1, r1, s2, r2, s3, r3, s4, r4, l4,
):
    g = lax.axis_index("grp")
    d = lax.axis_index("dev")
    y = d // 4
    xl = (d // 2) % 2
    c = d % 2
    half = x_ref.shape[0] // 2

    def idx(yy, xx):
        return yy * 4 + xx * 2 + c

    px = 1 - xl
    up, dn, op = (y + 1) % 4, (y + 3) % 4, (y + 2) % 4
    to_up, to_dn, to_x = (g, idx(up, xl)), (g, idx(dn, xl)), (g, idx(y, px))
    to_c = (g, y * 4 + xl * 2 + (1 - c))
    dev_peers = [(g, (d + i) % devs) for i in range(1, devs)]
    grp_peers = [((g + i) % grps, d) for i in range(1, grps)]
    greet(dev_peers + grp_peers)
    A, B = 0, 1
    rows = col_ref.shape[0] // grps

    def part_of(h):
        return x_ref.at[pl.ds(h * half, half)]

    def at(o, h):
        return y_ref.at[o, pl.ds(h * half, half)]

    def band(ref, i):
        return ref.at[pl.ds(pl.multiple_of(i * rows, rows), rows)]

    def lanes(ref, i):
        return ref.at[:, pl.ds(pl.multiple_of(i * 128, 128), 128)]

    mine = idx(y, xl)
    sends = []
    order = []

    def send(src, o, h, target, ssem, rsem):
        copy = remote(src, at(o, h), ssem, rsem, target)
        copy.start()
        sends.append(copy)

    def arrived(o, h, sem):
        remote(at(o, h), at(o, h), spare, sem, to_c).wait_recv()

    def across(src, o, h):
        i = len(order)
        order.append((o, h))
        send(src, o, h, to_c, cs.at[i], cr.at[i])

    own = pltpu.make_async_copy(x_ref, y_ref.at[mine], lsem)
    own.start()
    send(part_of(A), mine, A, to_dn, ds.at[0], ur.at[0])
    send(part_of(B), mine, B, to_up, us.at[0], dr.at[0])
    send(part_of(A), mine, A, to_x, xs.at[0], xr.at[0])
    send(part_of(B), mine, B, to_dn, ds.at[1], ur.at[1])
    send(part_of(A), mine, A, to_up, us.at[1], dr.at[1])
    send(part_of(B), mine, B, to_x, xs.at[1], xr.at[1])
    across(part_of(A), mine, A)
    across(part_of(B), mine, B)
    for peer in grp_peers:
        remote(band(col_ref, peer[0]), box1.at[g], s1, r1, peer).start()

    def settle(ref, count, ssem, rsem):
        whole = remote(ref.at[pl.ds(0, count)], ref.at[pl.ds(0, count)], ssem, rsem, to_c)
        whole.wait_send()
        whole.wait_recv()

    def round_two():
        settle(box1, grps - 1, s1, r1)
        box1[g] = band(col_ref, g)[...]
        total = box1[0]
        for i in range(1, grps):
            total = total + box1[i]
        part[...] = total
        for peer in dev_peers:
            remote(lanes(part, peer[1]), box2.at[d], s2, r2, peer).start()

    def round_three():
        settle(box2, devs - 1, s2, r2)
        box2[d] = lanes(part, d)[...]
        total = box2[0]
        for i in range(1, devs):
            total = total + box2[i]
        tile[...] = total
        for peer in dev_peers:
            remote(tile, full.at[d], s3, r3, peer).start()

    def round_four():
        settle(full, devs - 1, s3, r3)
        full[d] = tile[...]
        for i in range(devs):
            part[:, i * 128 : (i + 1) * 128] = full[i]
        for peer in grp_peers:
            remote(part, band(tot_ref, g), s4, r4, peer).start()
        last = pltpu.make_async_copy(part, band(tot_ref, g), l4)
        last.start()
        last.wait()

    steps = (
        (up, xl, A, ur, 0, to_dn, ds, ur, 2),
        (dn, xl, B, dr, 0, to_up, us, dr, 2),
        (y, px, A, xr, 0, to_dn, ds, ur, 3),
        (up, xl, B, ur, 1, to_x, xs, xr, 2),
        (dn, xl, A, dr, 1, to_x, xs, xr, 3),
        (y, px, B, xr, 1, to_up, us, dr, 3),
        (op, xl, A, ur, 2, None, None, None, 0),
        (op, xl, B, dr, 2, None, None, None, 0),
        (up, px, A, ur, 3, to_dn, ds, ur, 4),
        (dn, px, B, dr, 3, to_up, us, dr, 4),
        round_two,
        (up, px, B, xr, 2, None, None, None, 0),
        (dn, px, A, xr, 3, None, None, None, 0),
        round_three,
        (op, px, A, ur, 4, None, None, None, 0),
        (op, px, B, dr, 4, None, None, None, 0),
        round_four,
    )
    for step in steps:
        if callable(step):
            step()
            continue
        yy, xx, h, sems, i, target, ssems, rsems, j = step
        o = idx(yy, xx)
        arrived(o, h, sems.at[i])
        if target is not None:
            send(at(o, h), o, h, target, ssems.at[j], rsems.at[j])
        across(at(o, h), o, h)
    for i, (o, h) in enumerate(order):
        arrived(o + 1 - 2 * c, h, cr.at[i])
    for copy in sends:
        copy.wait_send()
    own.wait()
    others = tot_ref.at[pl.ds(0, rows * (grps - 1))]
    rest = remote(others, others, s4, r4, to_c)
    rest.wait_send()
    rest.wait_recv()


def gather_piece(x, col, grps, devs):
    sem = pltpu.SemaphoreType.DMA
    rows = col.shape[0] // grps
    vmem = pl.BlockSpec(memory_space=pltpu.VMEM)
    hbm = pl.BlockSpec(memory_space=pl.ANY)
    return pl.pallas_call(
        functools.partial(gather_kernel, grps, devs),
        out_shape=(
            jax.ShapeDtypeStruct((devs,) + x.shape, x.dtype),
            jax.ShapeDtypeStruct(col.shape, f32),
        ),
        in_specs=[hbm, vmem],
        out_specs=(hbm, vmem),
        scratch_shapes=[
            sem, sem((5,)), sem((5,)), sem((4,)), sem((16,)),
            sem((5,)), sem((5,)), sem((4,)), sem((16,)), sem,
            pltpu.VMEM((grps, rows, col.shape[1]), f32),
            pltpu.VMEM((rows, col.shape[1]), f32),
            pltpu.VMEM((devs, rows, 128), f32),
            pltpu.VMEM((rows, 128), f32),
            pltpu.VMEM((devs, rows, 128), f32),
            sem, sem, sem, sem, sem, sem, sem, sem, sem,
        ],
        compiler_params=pltpu.CompilerParams(collective_id=1, has_side_effects=True),
        name="gather_piece",
    )(x, col)


def finish_kernel(
    grps, devs, kv_ref, row_ref, box, rbox,
    other, total, cs, cr, ssem, rsem, s2, r2, lsem,
):
    g = lax.axis_index("grp")
    d = lax.axis_index("dev")
    y = d // 4
    c = d % 2
    chip = d // 2
    chips = devs // 2
    partner = (g, d + 1 - 2 * c)
    dev_peers = [(g, (d + i) % devs) for i in range(1, devs)]
    grp_peers = [((g + i) % grps, d) for i in range(1, grps)]
    greet(dev_peers + grp_peers)
    block = box.shape[1]
    span = 4 * block

    def rows(i, size):
        return pl.ds(pl.multiple_of(i * size, size), size)

    chunks = [(y + 2) % 4, (y + 1) % 4, (y + 3) % 4, y]
    swaps = []
    for i, j in enumerate(chunks):
        copy = remote(
            kv_ref.at[1 - c, rows(j, span)], other.at[rows(j, span)], cs.at[i], cr.at[i], partner
        )
        copy.start()
        swaps.append(copy)
    for peer in grp_peers:
        remote(row_ref, rbox.at[g], s2, r2, peer).start()
    for i, j in enumerate(chunks):
        swaps[i].wait_recv()
        at = rows(j, span)
        total[at, :] = (kv_ref[c, at, :].astype(f32) + other[at, :].astype(f32)).astype(bf16)
        for k in range(4):
            e = j * 4 + k
            src = total.at[rows(e, block)]
            if i < 3:
                remote(src, box.at[c * chips + chip], ssem, rsem, (g, e)).start()
            else:

                @pl.when(e != d)
                def _():
                    remote(src, box.at[c * chips + chip], ssem, rsem, (g, e)).start()

    mine = pltpu.make_async_copy(total.at[rows(d, block)], box.at[c * chips + chip], lsem)
    mine.start()
    mine.wait()
    for copy in swaps:
        copy.wait_send()
    some = rbox.at[pl.ds(0, grps - 1)]
    both = remote(some, some, s2, r2, partner)
    both.wait_send()
    both.wait_recv()
    rbox[g] = row_ref[...]
    some = box.at[pl.ds(0, devs - 1)]
    both = remote(some, some, ssem, rsem, partner)
    both.wait_send()
    both.wait_recv()


def totals_kernel(box, rbox, all_ref, key_ref, value_ref, first_ref, second_ref):
    chips = box.shape[0] // 2
    per = chips // KVH
    acc = rbox[0].astype(f32)
    for i in range(1, rbox.shape[0]):
        acc = acc + rbox[i].astype(f32)
    first_ref[...] = acc
    for kind, out in ((0, key_ref), (1, value_ref)):
        for m in range(KVH):
            acc = box[kind * chips + m * per].astype(f32)
            for i in range(1, per):
                acc = acc + box[kind * chips + m * per + i].astype(f32)
            out[:, m * HEAD_SIZE : (m + 1) * HEAD_SIZE] = acc
    second_ref[...] = all_ref[...]


def finish(kv, row, columns, grps, devs):
    piece = kv.shape[1]
    block = piece // devs
    sem = pltpu.SemaphoreType.DMA
    vmem = pl.BlockSpec(memory_space=pltpu.VMEM)
    box, rbox = pl.pallas_call(
        functools.partial(finish_kernel, grps, devs),
        out_shape=(
            jax.ShapeDtypeStruct((devs, block, HEAD_SIZE), bf16),
            jax.ShapeDtypeStruct((grps,) + row.shape, bf16),
        ),
        in_specs=[vmem, vmem],
        out_specs=(vmem, vmem),
        scratch_shapes=[
            pltpu.VMEM((piece, HEAD_SIZE), bf16),
            pltpu.VMEM((piece, HEAD_SIZE), bf16),
            sem((4,)), sem((4,)), sem, sem, sem, sem, sem,
        ],
        compiler_params=pltpu.CompilerParams(collective_id=3, has_side_effects=True),
        name="finish",
    )(kv, row)
    side = jax.ShapeDtypeStruct((block, KVH * HEAD_SIZE), f32)
    return pl.pallas_call(
        totals_kernel,
        out_shape=(
            side,
            side,
            jax.ShapeDtypeStruct(row.shape, f32),
            jax.ShapeDtypeStruct(columns.shape, f32),
        ),
        in_specs=[vmem, vmem, vmem],
        out_specs=(vmem, vmem, vmem, vmem),
        name="totals",
    )(box, rbox, columns)


BLOCK = 512


def forward_kernel(kv_ref, q_ref, k_ref, v_ref, f_ref, probs_ref, att_ref, fold_ref, scores, value_t):
    block = q_ref.shape[0]
    scale = HEAD_SIZE ** (-0.5)
    number = pl.program_id(1)

    @pl.when(jnp.logical_and(pl.program_id(0) == 0, number == 0))
    def _():
        value_t[...] = v_ref[...].astype(f32).T.astype(bf16)

    q = q_ref[...]
    above = lax.broadcasted_iota(jnp.int32, (block, block), 0) > lax.broadcasted_iota(
        jnp.int32, (block, block), 1
    )

    def rows(j):
        return pl.ds(pl.multiple_of(j * block, block), block)

    def score(j):
        return contraction(k_ref[rows(j), :], q, 1, 1) * scale

    def one(j, top):
        s = score(j)
        scores[rows(j), :] = s
        return jnp.maximum(top, jnp.max(s, axis=0, keepdims=True))

    s = jnp.where(above, neg_big, score(number))
    scores[rows(number), :] = s
    top = lax.fori_loop(0, number, one, jnp.max(s, axis=0, keepdims=True))

    def two(j, total):
        e = jnp.exp(scores[rows(j), :] - top)
        scores[rows(j), :] = e
        return total + jnp.sum(e, axis=0, keepdims=True)

    total = lax.fori_loop(0, number + 1, two, jnp.zeros((1, block), f32))
    share = 1.0 / total

    def three(j, acc):
        p = (scores[rows(j), :] * share).astype(bf16)
        probs_ref[0, 0, rows(j), :] = p
        return acc + jnp.dot(value_t[:, rows(j)], p, preferred_element_type=f32)

    acc = lax.fori_loop(0, number + 1, three, jnp.zeros((HEAD_SIZE, block), f32))
    att_ref[...] = acc.T.astype(bf16)
    fold = jnp.dot(f_ref[...], acc.astype(bf16), preferred_element_type=f32)
    fold = fold.astype(bf16).astype(f32)
    at = rows(number)

    @pl.when(pl.program_id(0) == 0)
    def _():
        fold_ref[:, at] = fold

    @pl.when(pl.program_id(0) > 0)
    def _():
        fold_ref[:, at] += fold


def attention_forward(kv_index, queries, keys, values, factor):
    piece, cols = queries.shape
    heads = cols // HEAD_SIZE
    blocks = piece // BLOCK
    grid_spec = pltpu.PrefetchScalarGridSpec(
        num_scalar_prefetch=1,
        grid=(heads, blocks),
        in_specs=[
            pl.BlockSpec((BLOCK, HEAD_SIZE), lambda h, i, kv: (i, h)),
            pl.BlockSpec((piece, HEAD_SIZE), lambda h, i, kv: (0, kv[0])),
            pl.BlockSpec((piece, HEAD_SIZE), lambda h, i, kv: (0, kv[0])),
            pl.BlockSpec((factor.shape[0], HEAD_SIZE), lambda h, i, kv: (0, h)),
        ],
        out_specs=(
            pl.BlockSpec((1, 1, piece, BLOCK), lambda h, i, kv: (h, i, 0, 0)),
            pl.BlockSpec((BLOCK, HEAD_SIZE), lambda h, i, kv: (i, h)),
            pl.BlockSpec((factor.shape[0], piece), lambda h, i, kv: (0, 0)),
        ),
        scratch_shapes=[pltpu.VMEM((piece, BLOCK), f32), pltpu.VMEM((HEAD_SIZE, piece), bf16)],
    )
    return pl.pallas_call(
        forward_kernel,
        grid_spec=grid_spec,
        out_shape=(
            jax.ShapeDtypeStruct((heads, blocks, piece, BLOCK), bf16),
            jax.ShapeDtypeStruct((piece, cols), bf16),
            jax.ShapeDtypeStruct((factor.shape[0], piece), f32),
        ),
        compiler_params=pltpu.CompilerParams(
            dimension_semantics=("arbitrary", "arbitrary"), vmem_limit_bytes=40 << 20
        ),
        cost_estimate=pl.CostEstimate(
            flops=20_000_000_000, bytes_accessed=40_000_000, transcendentals=5_000_000
        ),
        name="attention_forward",
    )(kv_index, queries, keys, values, factor)


def backward_kernel(
    kv_ref, p_ref, q_ref, seg_ref, att_ref, k_ref, v_ref, w_ref, f1_ref, f2_ref,
    dq_ref, kv_out, row_ref, key_t, key_sum, value_sum, grads, row_sum,
):
    block = q_ref.shape[0]
    scale = HEAD_SIZE ** (-0.5)
    number, head = pl.program_id(0), pl.program_id(1)
    heads = grads.shape[0]

    @pl.when(jnp.logical_and(head == 0, number == 0))
    def _():
        key_t[...] = k_ref[...].astype(f32).T.astype(bf16)
        key_sum[...] = jnp.zeros_like(key_sum)
        value_sum[...] = jnp.zeros_like(value_sum)
        row_sum[...] = jnp.zeros_like(row_sum)

    @pl.when(head == 0)
    def _():
        seg = seg_ref[...]
        low = contraction(seg, f2_ref[...], 1, 1).astype(bf16)
        full = contraction(seg, w_ref[...], 1, 1) + adapter_scale * jnp.dot(
            low, f1_ref[...], preferred_element_type=f32
        )
        for h in range(heads):
            grads[h] = full[:, h * HEAD_SIZE : (h + 1) * HEAD_SIZE].astype(bf16)
        row_sum[...] += contraction(low, att_ref[...], 0, 0)

    q = q_ref[...]
    g = grads[head]
    att = att_ref[:, pl.ds(pl.multiple_of(head * HEAD_SIZE, HEAD_SIZE), HEAD_SIZE)]
    delta = jnp.sum((g.astype(f32) * att.astype(f32)).T, axis=0, keepdims=True)

    def rows(j):
        return pl.ds(pl.multiple_of(j * block, block), block)

    def turn(j, acc):
        p = p_ref[0, 0, rows(j), :]
        grad = contraction(v_ref[rows(j), :], g, 1, 1)
        ds = (p.astype(f32) * (grad - delta)).astype(bf16)
        value_sum[rows(j), :] += jnp.dot(p, g, preferred_element_type=f32)
        key_sum[rows(j), :] += jnp.dot(ds, q, preferred_element_type=f32)
        return acc + jnp.dot(key_t[:, rows(j)], ds, preferred_element_type=f32)

    acc = lax.fori_loop(0, number + 1, turn, jnp.zeros((HEAD_SIZE, block), f32))
    dq_ref[...] = acc.T * scale

    @pl.when(jnp.logical_and(head == pl.num_programs(1) - 1, number == pl.num_programs(0) - 1))
    def _():
        kv_out[0] = (key_sum[...] * scale).astype(bf16)
        kv_out[1] = value_sum[...].astype(bf16)
        row_ref[...] = (adapter_scale * row_sum[...]).astype(bf16)


def attention_backward(kv_index, probs, queries, segment, attended, keys, values, weight, first, second):
    piece, cols = queries.shape
    heads = cols // HEAD_SIZE
    blocks = piece // BLOCK
    once = pl.Buffered(1)
    tile = pl.BlockSpec((BLOCK, HEAD_SIZE), lambda i, h, kv: (i, h))
    column = pl.BlockSpec((piece, HEAD_SIZE), lambda i, h, kv: (0, kv[0]), pipeline_mode=once)
    whole = lambda a: pl.BlockSpec(a.shape, lambda i, h, kv: (0, 0), pipeline_mode=once)
    grid_spec = pltpu.PrefetchScalarGridSpec(
        num_scalar_prefetch=1,
        grid=(blocks, heads),
        in_specs=[
            pl.BlockSpec((1, 1, piece, BLOCK), lambda i, h, kv: (h, i, 0, 0)),
            tile,
            pl.BlockSpec((BLOCK, segment.shape[1]), lambda i, h, kv: (i, 0)),
            pl.BlockSpec((BLOCK, cols), lambda i, h, kv: (i, 0)),
            column,
            column,
            whole(weight),
            whole(first),
            whole(second),
        ],
        out_specs=(
            tile,
            pl.BlockSpec((2, piece, HEAD_SIZE), lambda i, h, kv: (0, 0, 0)),
            pl.BlockSpec(first.shape, lambda i, h, kv: (0, 0)),
        ),
        scratch_shapes=[
            pltpu.VMEM((HEAD_SIZE, piece), bf16),
            pltpu.VMEM((piece, HEAD_SIZE), f32),
            pltpu.VMEM((piece, HEAD_SIZE), f32),
            pltpu.VMEM((heads, BLOCK, HEAD_SIZE), bf16),
            pltpu.VMEM(first.shape, f32),
        ],
    )
    return pl.pallas_call(
        backward_kernel,
        grid_spec=grid_spec,
        out_shape=(
            jax.ShapeDtypeStruct((piece, cols), f32),
            jax.ShapeDtypeStruct((2, piece, HEAD_SIZE), bf16),
            jax.ShapeDtypeStruct(first.shape, bf16),
        ),
        compiler_params=pltpu.CompilerParams(
            dimension_semantics=("arbitrary", "arbitrary"), vmem_limit_bytes=48 << 20
        ),
        cost_estimate=pl.CostEstimate(
            flops=20_000_000_000, bytes_accessed=40_000_000, transcendentals=0
        ),
        name="attention_backward",
    )(kv_index, probs, queries, segment, attended, keys, values, weight, first, second)


def exchange(x, axes):
    return lax.all_to_all(x, axes, split_axis=0, concat_axis=0, tiled=True)


def on_device(
    output_gradient,
    expert_choice_index,
    routing_weight,
    stored_gate_preact,
    gate_up_weight,
    down_weight,
    down_first_factor,
    down_second_factor,
    rotated_queries,
    rotated_keys,
    stored_values,
    output_weight,
    output_first_factor,
    output_second_factor,
):
    tok_rows, model_width = output_gradient.shape
    grp_count = lax.axis_size("grp")
    dev_count = lax.axis_size("dev")
    experts = grp_count * dev_count
    slot_count = stored_gate_preact.shape[1]
    capacity = slot_count // experts
    sub = model_width // 128
    piece_len, share_cols = rotated_queries.shape
    device_share = share_cols // HEAD_SIZE
    group_size = QUERY_HEADS // KVH
    kv_index = (lax.axis_index("dev") * device_share // group_size).astype(jnp.int32).reshape(1)

    outgoing, cells = dispatch(
        output_gradient, expert_choice_index, routing_weight, experts, capacity
    )
    incoming = exchange(outgoing.reshape(experts, capacity, sub, 128), ALL)
    probs, attended, folded = attention_forward(
        kv_index, rotated_queries, rotated_keys, stored_values, output_first_factor
    )
    share = share_tokens(folded, dev_count)

    grad_rows, gradient_first, gradient_second = experts_backward(
        incoming.reshape(slot_count, sub, 128),
        stored_gate_preact[0],
        gate_up_weight[0],
        down_weight[0],
        down_first_factor[0],
        down_second_factor[0],
        256,
    )
    returned = exchange(grad_rows.reshape(experts, capacity, sub, 128), ALL)
    residual_gradient, column_contrib = combine(
        cells,
        output_gradient,
        returned.reshape(slot_count, sub, 128),
        share,
    )
    segment_gradient, columns = gather_piece(
        residual_gradient, column_contrib, grp_count, dev_count
    )
    query_gradient, kv_terms, row_contrib = attention_backward(
        kv_index,
        probs,
        rotated_queries,
        segment_gradient.reshape(piece_len, model_width),
        attended,
        rotated_keys,
        stored_values,
        output_weight,
        output_first_factor,
        output_second_factor,
    )
    key_gradient, value_gradient, output_first_gradient, output_second_gradient = finish(
        kv_terms, row_contrib, columns, grp_count, dev_count
    )
    return (
        gradient_first[None],
        gradient_second[None],
        residual_gradient,
        output_first_gradient,
        output_second_gradient,
        query_gradient,
        key_gradient,
        value_gradient,
    )


def solution(mesh):
    in_specs = (
        P(("grp", "dev"), None),
        P(("grp", "dev"), None),
        P(("grp", "dev"), None),
        P(("grp", "dev"), None, None),
        P(("grp", "dev"), None, None),
        P(("grp", "dev"), None, None),
        P(("grp", "dev"), None, None),
        P(("grp", "dev"), None, None),
        P("grp", "dev"),
        P("grp", None),
        P("grp", None),
        P("dev", None),
        P(None, "dev"),
        P(),
    )
    out_specs = (
        P(("grp", "dev"), None, None),
        P(("grp", "dev"), None, None),
        P(("grp", "dev"), None),
        P(None, "dev"),
        P(),
        P("grp", "dev"),
        P(("grp", "dev"), None),
        P(("grp", "dev"), None),
    )
    return jax.shard_map(
        on_device, mesh=mesh, in_specs=in_specs, out_specs=out_specs, check_vma=False
    )
```
